256 devices in a mesh: outer: 8 (over x_hi, y), inner: 32 (over x_lo, z, core).
Axes of the slice: x: 4 (x_hi: 2, x_lo: 2; x = x_hi * 2 + x_lo), y: 4, z: 8, core: 2. Of those that a mesh axis runs over, the one named last changes fastest.
Arguments:
- vectors: bfloat16 [524288, 256], P(('outer', 'inner')), may hold values from -6 to 6
- leaf_basis: bfloat16 [524288, 256], P(('outer', 'inner')), may hold values from -0.375 to 0.375
- transfer: bfloat16 [4, 8, 32, 8, 512, 256], P(None, 'outer', 'inner'), may hold values from -0.25 to 0.25
- core_mats: bfloat16 [8, 32, 8, 256, 256], P('outer', 'inner'), may hold values from -0.375 to 0.375
- row_basis: bfloat16 [524288, 256], P(('outer', 'inner')), may hold values from -0.375 to 0.375
- box_order: int32 [8, 32, 8], P('outer', 'inner'), may hold values from 0 to 7, each once within a row
Outputs:
- applied: bfloat16 [524288, 256], P(('outer', 'inner'))
The draws below stay inside these ranges and needn't reach their ends.
Inputs may be any that keep to these rules, and one draw needn't show every extreme that they name: `box_order`: for every device the 8 entries are a permutation of 0 to 7.
All inputs are finite; a program needn't handle non-finite values.
Results may differ from the reference program's by a relative error of at most 0.011.
Values may be sent and summed in bfloat16 or wider, within the bound.
A program may use at most 64 MiB of HBM per device.

```python
import jax
import jax.numpy as jnp
from jax import lax

R = 256
BOX_DEV = 8
LEVELS = 4
LEAF = 256
C = 256
ROWS = 524288
N_OUTER = 8
N_INNER = 32


def level_of(own_key, extent, cuts, low, top_value):
    def one(dim, parts):
        heights = jax.random.uniform(jax.random.fold_in(jax.random.fold_in(own_key, 6), dim), (parts,), jnp.float32, low / len(cuts), top_value / len(cuts))
        return jnp.repeat(jnp.exp(heights), extent[dim] // parts).reshape((-1,) + (1,) * (len(extent) - dim - 1))

    factor_of = one(*cuts[0])
    for cut in cuts[1:]:
        factor_of = factor_of * one(*cut)
    return factor_of


def noise(rng, dims, deviation, reach, cuts=(), kind=jnp.bfloat16):
    entries = deviation * jax.random.normal(rng, dims, jnp.float32)
    if cuts:
        entries = entries * level_of(rng, dims, cuts, -0.22, 0.18)
    return jnp.clip(entries, -reach, reach).astype(kind)


def setup_inputs(seed: int = 0) -> dict:
    splits = jax.random.split(jax.random.key(seed), 7)
    return {
        "vectors": noise(splits[0], (ROWS, C), 1.0, 6.0, ((0, 256),)),
        "leaf_basis": noise(splits[1], (ROWS, R), LEAF ** -0.5, 0.375, ((0, 256),)),
        "transfer": noise(splits[2], (LEVELS, N_OUTER, N_INNER, BOX_DEV, 2 * R, R), (2 * R) ** -0.5, 0.25, ((1, 8), (2, 32))),
        "core_mats": noise(splits[3], (N_OUTER, N_INNER, BOX_DEV, R, R), R ** -0.5, 0.375, ((0, 8), (1, 32))),
        "row_basis": noise(splits[4], (ROWS, R), R ** -0.5, 0.375, ((0, 256),)),
        "box_order": jax.vmap(lambda own: jax.random.permutation(own, BOX_DEV))(jax.random.split(splits[5], N_OUTER * N_INNER)).reshape((N_OUTER, N_INNER, BOX_DEV)).astype(jnp.int32),
    }


def widen(values):
    return lax.optimization_barrier(values).astype(jnp.float32)


def reference(vectors, leaf_basis, transfer, core_mats, row_basis, box_order):
    dev_count = N_OUTER * N_INNER
    half_count = BOX_DEV // 2
    x_boxes = vectors.reshape(dev_count, BOX_DEV, LEAF, C).astype(jnp.float32)
    v_boxes = leaf_basis.reshape(dev_count, BOX_DEV, LEAF, R).astype(jnp.float32)
    box_state = jnp.einsum('dklc,dklr->dkcr', x_boxes, v_boxes).astype(jnp.bfloat16)
    weights = transfer.reshape(LEVELS, dev_count, half_count, 2, 2 * R, R)
    device_ids = jnp.arange(dev_count, dtype=jnp.int32)
    inner_bits = N_INNER.bit_length() - 1
    bit_list = [0, 1, inner_bits, inner_bits + 1]
    for level_idx in range(LEVELS):
        bit_pos = bit_list[level_idx]
        partner = jnp.bitwise_xor(device_ids, jnp.int32(1 << bit_pos))
        half_flag = jnp.bitwise_and(jnp.right_shift(device_ids, jnp.int32(bit_pos)), jnp.int32(1))
        low_dev = jnp.where(half_flag == 0, device_ids, partner)
        high_dev = jnp.where(half_flag == 0, partner, device_ids)
        halves = box_state.reshape(dev_count, 2, half_count, C, R)
        low_half = halves[low_dev, half_flag]
        high_half = halves[high_dev, half_flag]
        stacked = widen(jnp.concatenate([low_half, high_half], axis=3))
        level_w = weights[level_idx].astype(jnp.float32)
        merged = jnp.einsum('dkcs,dkosr->dkocr', stacked, level_w)
        box_state = merged.reshape(dev_count, BOX_DEV, C, R).astype(jnp.bfloat16)
    slot_order = box_order.reshape(dev_count, BOX_DEV)
    chosen = widen(jnp.take_along_axis(box_state, slot_order[:, :, None, None], axis=1))
    cores = core_mats.reshape(dev_count, BOX_DEV, R, R).astype(jnp.float32)
    core_out = jnp.einsum('dkcs,dksr->dkcr', chosen, cores).astype(jnp.bfloat16)
    u_boxes = row_basis.reshape(dev_count, BOX_DEV, LEAF, R).astype(jnp.float32)
    boxed = jnp.einsum('dklr,dkcr->dklc', u_boxes, widen(core_out)).astype(jnp.bfloat16)
    piece_rows = BOX_DEV * LEAF // N_INNER
    placed = boxed.reshape(N_OUTER, N_INNER, N_INNER, piece_rows, C).transpose(0, 2, 1, 3, 4)
    return placed.reshape(ROWS, C)
```

```python
import functools

import jax
import jax.numpy as jnp
from jax import lax
from jax.experimental import pallas as pl
from jax.experimental.pallas import tpu as pltpu
from jax.sharding import PartitionSpec as P

MESH = pl.DeviceIdType.MESH
F32 = jnp.float32
BF16 = jnp.bfloat16
LEVELS = 4
BOXES = 8
HALF = 4
RANK = 256
LEAF = 256
COLS = 256
CHUNKS = 4
WIDTH = COLS // CHUNKS
PEERS = 32
PIECE = BOXES * LEAF // PEERS

ORDER = (
    (0, 0), (0, 1), (0, 2), (0, 3),
    (1, 0), (1, 1), (2, 0), (1, 2), (2, 1), (1, 3),
    (3, 0), (2, 2), (3, 1), (2, 3), (3, 2), (3, 3),
)


def kernel(
    x_hbm, v_hbm, t_hbm, c_hbm, u_hbm, order_ref, out_ref,
    xv, vv, tv, cv, uv, s0, s1, s2, s3, s4, r0, r1, r2, r3, bx, rb,
    in_sem, lev_send, lev_recv, far_send, far_recv,
):
    outer = lax.axis_index("outer")
    inner = lax.axis_index("inner")
    states = (s0, s1, s2, s3, s4)
    arrivals = (r0, r1, r2, r3)

    def bit(value, place):
        return lax.rem(lax.div(value, 1 << place), 2)

    flags = (bit(inner, 0), bit(inner, 1), bit(outer, 0), bit(outer, 1))
    partners = (
        (outer, inner + (1 - 2 * flags[0])),
        (outer, inner + 2 * (1 - 2 * flags[1])),
        (outer + (1 - 2 * flags[2]), inner),
        (outer + 2 * (1 - 2 * flags[3]), inner),
    )

    my_box = lax.div(inner, HALF)
    my_quarter = lax.rem(inner, HALF)
    my_x = lax.div(my_box, 4)
    my_pair = lax.rem(my_box, 4)
    boxes_order = []
    for pair_step in (2, 1, 3, 0):
        for x_step in (1, 0):
            box = lax.rem(my_x + x_step, 2) * 4 + lax.rem(my_pair + pair_step, 4)
            quarters = []
            for step in (1, 2, 3, 0):
                quarter = lax.rem(my_quarter + step, 4)
                is_self = pair_step == 0 and x_step == 0 and step == 0
                quarters.append((quarter, is_self))
            boxes_order.append((box, quarters))

    loads = [
        pltpu.make_async_copy(src, dst, in_sem.at[n])
        for n, (src, dst) in enumerate(
            (
                (x_hbm, xv), (v_hbm, vv),
                (t_hbm.at[0], tv.at[0]), (t_hbm.at[1], tv.at[1]),
                (t_hbm.at[2], tv.at[2]), (t_hbm.at[3], tv.at[3]),
                (c_hbm, cv), (u_hbm, uv),
            )
        )
    ]
    for load in loads:
        load.start()

    barrier = pltpu.get_barrier_semaphore()
    greeted = 0
    for box, quarters in boxes_order:
        for quarter, is_self in quarters:
            if not is_self:
                pl.semaphore_signal(
                    barrier, inc=1, device_id=(outer, box * 4 + quarter), device_id_type=MESH
                )
                greeted += 1
    for partner in partners[2:]:
        pl.semaphore_signal(barrier, inc=1, device_id=partner, device_id_type=MESH)
        greeted += 1

    def level_copy(level, chunk):
        return pltpu.make_async_remote_copy(
            src_ref=states[level].at[chunk, pl.ds((1 - flags[level]) * HALF, HALF)],
            dst_ref=arrivals[level].at[chunk],
            send_sem=lev_send.at[level, chunk],
            recv_sem=lev_recv.at[level, chunk],
            device_id=partners[level],
            device_id_type=MESH,
        )

    def leaf(box):
        rows = pl.ds(pl.multiple_of(box * LEAF, LEAF), LEAF)
        made = lax.dot_general(
            xv[rows, :], vv[rows, :], (((0,), (0,)), ((), ())), preferred_element_type=F32
        ).astype(BF16)
        for chunk in range(CHUNKS):
            s0[chunk, box] = made[chunk * WIDTH : (chunk + 1) * WIDTH]

    loads[0].wait()
    loads[1].wait()
    for n in range(HALF):
        leaf((1 - flags[0]) * HALF + n)
    pl.semaphore_wait(barrier, greeted)
    for chunk in range(CHUNKS):
        level_copy(0, chunk).start()
    for n in range(HALF):
        leaf(flags[0] * HALF + n)

    def merge(level, chunk, pair):
        flag = flags[level]
        kept = states[level][chunk, flag * HALF + pair]
        came = arrivals[level][chunk, pair]
        for o in range(2):
            box = 2 * pair + o
            kept_w = tv[level, box, pl.ds(pl.multiple_of(flag * RANK, RANK), RANK), :]
            came_w = tv[level, box, pl.ds(pl.multiple_of((1 - flag) * RANK, RANK), RANK), :]
            total = jnp.dot(kept, kept_w, preferred_element_type=F32)
            total = total + jnp.dot(came, came_w, preferred_element_type=F32)
            states[level + 1][chunk, box] = total.astype(BF16)

    def far_copy(chunk, box, quarter):
        peer = box * 4 + quarter
        return pltpu.make_async_remote_copy(
            src_ref=bx.at[chunk, peer],
            dst_ref=rb.at[chunk, inner],
            send_sem=far_send.at[chunk, peer],
            recv_sem=far_recv.at[chunk, inner],
            device_id=(outer, peer),
            device_id_type=MESH,
        )

    def far_arrival(chunk, peer):
        return pltpu.make_async_remote_copy(
            src_ref=bx.at[chunk, peer],
            dst_ref=rb.at[chunk, peer],
            send_sem=far_send.at[chunk, peer],
            recv_sem=far_recv.at[chunk, peer],
            device_id=(outer, peer),
            device_id_type=MESH,
        )

    def finish(chunk):
        for box, quarters in boxes_order:
            chosen = s4[chunk, order_ref[box]]
            core = jnp.dot(chosen, cv[box], preferred_element_type=F32).astype(BF16)
            rows = pl.ds(pl.multiple_of(box * LEAF, LEAF), LEAF)
            made = lax.dot_general(
                uv[rows, :], core, (((1,), (1,)), ((), ())), preferred_element_type=F32
            )
            for quarter in range(4):
                at = quarter * PIECE
                packed = jnp.concatenate(
                    [made[at : at + PIECE // 2], made[at + PIECE // 2 : at + PIECE]], axis=1
                ).astype(BF16)
                bx[chunk, box * 4 + quarter] = packed
            for quarter, is_self in quarters:
                if is_self:
                    rb[chunk, inner] = bx[chunk, inner]
                else:
                    far_copy(chunk, box, quarter).start()

    waited = set()
    for level, chunk in ORDER:
        if level not in waited:
            waited.add(level)
            loads[2 + level].wait()
        copy = level_copy(level, chunk)
        copy.wait()
        if level < LEVELS - 1:
            later = flags[level + 1]
            for n in range(2):
                merge(level, chunk, (1 - later) * 2 + n)
            level_copy(level + 1, chunk).start()
            for n in range(2):
                merge(level, chunk, later * 2 + n)
        else:
            for n in range(HALF):
                merge(level, chunk, n)
            if chunk == 0:
                loads[6].wait()
                loads[7].wait()
            finish(chunk)

    lane = lax.broadcasted_iota(jnp.int32, (PIECE // 2, 128), 1)
    for duo in range(CHUNKS // 2):
        for chunk in (2 * duo, 2 * duo + 1):
            for box, quarters in boxes_order:
                for quarter, is_self in quarters:
                    if not is_self:
                        far_arrival(chunk, box * 4 + quarter).wait()

        def unpack(peer, carry):
            first = rb[2 * duo, peer].astype(F32)
            second = rb[2 * duo + 1, peer].astype(F32)
            low = jnp.where(lane < WIDTH, first, pltpu.roll(second, WIDTH, 1))
            high = jnp.where(lane < WIDTH, pltpu.roll(first, WIDTH, 1), second)
            base = pl.multiple_of(peer * PIECE, PIECE)
            cols = slice(duo * 128, duo * 128 + 128)
            out_ref[pl.ds(base, PIECE // 2), cols] = low.astype(BF16)
            out_ref[pl.ds(base + PIECE // 2, PIECE // 2), cols] = high.astype(BF16)
            return carry

        lax.fori_loop(0, PEERS, unpack, 0)


def on_device(vectors, leaf_basis, transfer, core_mats, row_basis, box_order):
    any_space = pl.BlockSpec(memory_space=pl.ANY)
    call = pl.pallas_call(
        kernel,
        out_shape=jax.ShapeDtypeStruct((BOXES * LEAF, COLS), BF16),
        in_specs=[any_space] * 5 + [pl.BlockSpec(memory_space=pltpu.SMEM)],
        out_specs=pl.BlockSpec(memory_space=pltpu.VMEM),
        scratch_shapes=[
            pltpu.VMEM((BOXES * LEAF, COLS), BF16),
            pltpu.VMEM((BOXES * LEAF, RANK), BF16),
            pltpu.VMEM((LEVELS, BOXES, 2 * RANK, RANK), BF16),
            pltpu.VMEM((BOXES, RANK, RANK), BF16),
            pltpu.VMEM((BOXES * LEAF, RANK), BF16),
        ]
        + [pltpu.VMEM((CHUNKS, BOXES, WIDTH, RANK), BF16)] * 5
        + [pltpu.VMEM((CHUNKS, HALF, WIDTH, RANK), BF16)] * 4
        + [
            pltpu.VMEM((CHUNKS, PEERS, PIECE // 2, 128), BF16),
            pltpu.VMEM((CHUNKS, PEERS, PIECE // 2, 128), BF16),
            pltpu.SemaphoreType.DMA((8,)),
            pltpu.SemaphoreType.DMA((LEVELS, CHUNKS)),
            pltpu.SemaphoreType.DMA((LEVELS, CHUNKS)),
            pltpu.SemaphoreType.DMA((CHUNKS, PEERS)),
            pltpu.SemaphoreType.DMA((CHUNKS, PEERS)),
        ],
        compiler_params=pltpu.CompilerParams(
            collective_id=0, has_side_effects=True, vmem_limit_bytes=60 * 1024 * 1024
        ),
        name="butterfly",
    )
    return call(
        vectors,
        leaf_basis,
        transfer.reshape(LEVELS, BOXES, 2 * RANK, RANK),
        core_mats.reshape(BOXES, RANK, RANK),
        row_basis,
        box_order.reshape(BOXES),
    )


def solution(mesh):
    in_specs = (
        P(("outer", "inner"), None),
        P(("outer", "inner"), None),
        P(None, "outer", "inner", None, None, None),
        P("outer", "inner", None, None, None),
        P(("outer", "inner"), None),
        P("outer", "inner", None),
    )
    out_specs = P(("outer", "inner"), None)
    return jax.shard_map(
        on_device, mesh=mesh, in_specs=in_specs, out_specs=out_specs, check_vma=False
    )
```

```python
import functools

import jax
import jax.numpy as jnp
from jax import lax
from jax.experimental import pallas as pl
from jax.experimental.pallas import tpu as pltpu
from jax.sharding import PartitionSpec as P

MESH = pl.DeviceIdType.MESH
F32 = jnp.float32
BF16 = jnp.bfloat16
LEVELS = 4
BOXES = 8
HALF = 4
RANK = 256
LEAF = 256
COLS = 256
CHUNKS = ((0, 32), (64, 64), (128, 64), (192, 64), (32, 32))
COUNT = len(CHUNKS)
LANES = 128
KERNEL_VMEM = 65_600_000
PEERS = 32
PIECE = BOXES * LEAF // PEERS
PIECE_ROWS = tuple(PIECE * width // LANES for _, width in CHUNKS)
PIECE_AT = tuple(sum(PIECE_ROWS[:c]) for c in range(COUNT))
ALL_ROWS = sum(PIECE_ROWS)

STEPS = (
    ("m", 0, 0, 0), ("s", 1, 0), ("m", 0, 0, 1), ("m", 0, 1, 0), ("s", 1, 1), ("m", 0, 1, 1),
    ("m", 0, 2, 0), ("s", 1, 2), ("m", 0, 2, 1), ("m", 0, 3, 0), ("s", 1, 3), ("m", 0, 3, 1),
    ("m", 0, 4, 0), ("s", 1, 4), ("m", 0, 4, 1), ("m", 1, 0, 0), ("s", 2, 0), ("m", 1, 0, 1),
    ("m", 2, 0, 0), ("s", 3, 0), ("m", 1, 1, 0), ("s", 2, 1), ("m", 1, 1, 1), ("m", 2, 0, 1),
    ("m", 1, 2, 0), ("m", 1, 2, 1), ("m", 2, 1, 0), ("s", 3, 1), ("s", 2, 2), ("m", 3, 0, 0),
    ("m", 3, 0, 1), ("f", 0), ("m", 2, 1, 1), ("m", 1, 3, 0), ("m", 1, 3, 1), ("m", 1, 4, 0),
    ("m", 1, 4, 1), ("m", 2, 2, 0), ("s", 3, 2), ("s", 2, 3), ("m", 3, 1, 0), ("m", 3, 1, 1),
    ("f", 1), ("m", 2, 2, 1), ("m", 2, 3, 0), ("s", 3, 3), ("s", 2, 4), ("m", 3, 2, 0),
    ("m", 3, 2, 1), ("f", 2), ("m", 2, 3, 1), ("m", 2, 4, 0), ("s", 3, 4), ("m", 3, 3, 0),
    ("m", 3, 3, 1), ("f", 3), ("m", 2, 4, 1), ("m", 3, 4, 0), ("m", 3, 4, 1), ("f", 4),
)


def kernel(
    x_hbm, v_hbm, t_hbm, c_hbm, u_hbm, order_ref, rb,
    xv, vv, tv, cv, uv, bx, *rest,
):
    outer = lax.axis_index("outer")
    inner = lax.axis_index("inner")
    rest = list(rest)

    def take(count):
        taken, rest[:] = rest[:count], rest[count:]
        return taken

    states = [take(COUNT) for _ in range(LEVELS + 1)]
    arrivals = [take(COUNT) for _ in range(LEVELS)]
    cores = take(COUNT)
    in_sem, own_sem, lev_send, lev_recv, far_send, far_recv = rest

    def bit(value, place):
        return lax.rem(lax.div(value, 1 << place), 2)

    flags = (bit(inner, 0), bit(inner, 1), bit(outer, 0), bit(outer, 1))
    partners = (
        (outer, inner + (1 - 2 * flags[0])),
        (outer, inner + 2 * (1 - 2 * flags[1])),
        (outer + (1 - 2 * flags[2]), inner),
        (outer + 2 * (1 - 2 * flags[3]), inner),
    )

    my_box = lax.div(inner, HALF)
    my_quarter = lax.rem(inner, HALF)
    my_x = lax.div(my_box, 4)
    my_pair = lax.rem(my_box, 4)
    boxes_order = []
    for pair_step in (2, 1, 3, 0):
        for x_step in (1, 0):
            box = lax.rem(my_x + x_step, 2) * 4 + lax.rem(my_pair + pair_step, 4)
            quarters = []
            for step in (1, 2, 3, 0):
                quarter = lax.rem(my_quarter + step, 4)
                is_self = pair_step == 0 and x_step == 0 and step == 0
                quarters.append((quarter, is_self))
            boxes_order.append((box, quarters))

    def half_rows(side):
        return pl.ds(pl.multiple_of(side * (HALF * LEAF), HALF * LEAF), HALF * LEAF)

    sent_rows, kept_rows = half_rows(1 - flags[0]), half_rows(flags[0])
    loads = [
        pltpu.make_async_copy(src, dst, in_sem.at[n])
        for n, (src, dst) in enumerate(
            (
                (t_hbm.at[0], tv.at[0]), (t_hbm.at[1], tv.at[1]),
                (t_hbm.at[2], tv.at[2]), (t_hbm.at[3], tv.at[3]),
                (c_hbm, cv), (u_hbm, uv),
                (x_hbm.at[sent_rows], xv.at[sent_rows]), (v_hbm.at[sent_rows], vv.at[sent_rows]),
                (x_hbm.at[kept_rows], xv.at[kept_rows]), (v_hbm.at[kept_rows], vv.at[kept_rows]),
            )
        )
    ]
    for n in (6, 7):
        loads[n].start()

    barrier = pltpu.get_barrier_semaphore()
    greeted = 0
    for box, quarters in boxes_order:
        for quarter, is_self in quarters:
            if not is_self:
                pl.semaphore_signal(
                    barrier, inc=1, device_id=(outer, box * 4 + quarter), device_id_type=MESH
                )
                greeted += 1
    for partner in partners[2:]:
        pl.semaphore_signal(barrier, inc=1, device_id=partner, device_id_type=MESH)
        greeted += 1

    def first_pair(level, half):
        if level < LEVELS - 1:
            later = flags[level + 1]
            return 2 * (1 - later) if half == 0 else 2 * later
        return 2 * half

    def level_copy(level, chunk, half):
        halves = level in (1, 2)
        at, size = (first_pair(level, half), 2) if halves else (0, HALF)
        return pltpu.make_async_remote_copy(
            src_ref=states[level][chunk].at[pl.ds((1 - flags[level]) * HALF + at, size)],
            dst_ref=arrivals[level][chunk].at[pl.ds(at, size)],
            send_sem=lev_send.at[level, chunk],
            recv_sem=lev_recv.at[level, chunk, half],
            device_id=partners[level],
            device_id_type=MESH,
        )

    def send(level, chunk):
        level_copy(level, chunk, 0).start()
        if level in (1, 2):
            level_copy(level, chunk, 1).start()

    def leaf(box):
        rows = pl.ds(pl.multiple_of(box * LEAF, LEAF), LEAF)
        made = lax.dot_general(
            xv[rows, :], vv[rows, :], (((0,), (0,)), ((), ())), preferred_element_type=F32
        ).astype(BF16)
        for chunk, (at, width) in enumerate(CHUNKS):
            states[0][chunk][box] = made[at : at + width]

    with jax.named_scope("load"):
        loads[6].wait()
        loads[7].wait()
    for n in (8, 9, 0):
        loads[n].start()
    for n in range(HALF):
        leaf((1 - flags[0]) * HALF + n)
    with jax.named_scope("greet"):
        pl.semaphore_wait(barrier, greeted)
    for chunk in range(COUNT):
        send(0, chunk)
    for n in (1, 2, 3, 4, 5):
        loads[n].start()
    loads[8].wait()
    loads[9].wait()
    for n in range(HALF):
        leaf(flags[0] * HALF + n)

    def merge(level, chunk, pair):
        flag = flags[level]
        kept = states[level][chunk][flag * HALF + pair]
        came = arrivals[level][chunk][pair]
        for o in range(2):
            box = 2 * pair + o
            kept_w = tv[level, box, pl.ds(pl.multiple_of(flag * RANK, RANK), RANK), :]
            came_w = tv[level, box, pl.ds(pl.multiple_of((1 - flag) * RANK, RANK), RANK), :]
            total = jnp.dot(kept, kept_w, preferred_element_type=F32)
            total = total + jnp.dot(came, came_w, preferred_element_type=F32)
            states[level + 1][chunk][box] = total.astype(BF16)

    def far_copy(chunk, box, quarter):
        peer = box * 4 + quarter
        rows = pl.ds(PIECE_AT[chunk], PIECE_ROWS[chunk])
        return pltpu.make_async_remote_copy(
            src_ref=bx.at[peer, rows],
            dst_ref=rb.at[inner, rows],
            send_sem=far_send.at[0],
            recv_sem=far_recv.at[chunk],
            device_id=(outer, peer),
            device_id_type=MESH,
        )

    own = [
        pltpu.make_async_copy(
            bx.at[inner, pl.ds(at, rows)], rb.at[inner, pl.ds(at, rows)], own_sem.at[0]
        )
        for at, rows in zip(PIECE_AT, PIECE_ROWS)
    ]

    def finish(chunk):
        size = PIECE_ROWS[chunk]
        at = PIECE_AT[chunk]
        core = cores[chunk]
        for box, _ in boxes_order:
            core[box] = jnp.dot(
                states[LEVELS][chunk][order_ref[box]], cv[box], preferred_element_type=F32
            ).astype(BF16)
        for box, quarters in boxes_order:
            rows = pl.ds(pl.multiple_of(box * LEAF, LEAF), LEAF)
            made = jnp.dot(uv[rows, :], core[box].T, preferred_element_type=F32)
            for quarter in range(4):
                groups = [
                    made[first : first + size]
                    for first in range(quarter * PIECE, (quarter + 1) * PIECE, size)
                ]
                bx[box * 4 + quarter, at : at + size] = jnp.concatenate(groups, axis=1).astype(BF16)
        with jax.named_scope("go"):
            for box, quarters in boxes_order:
                for quarter, is_self in quarters:
                    if is_self:
                        own[chunk].start()
                    else:
                        far_copy(chunk, box, quarter).start()

    loaded = set()

    def need(n):
        if n not in loaded:
            loaded.add(n)
            loads[n].wait()

    for kind, *numbers in STEPS:
        if kind == "m":
            level, chunk, half = numbers
            need(level)
            if half == 0 or level in (1, 2):
                with jax.named_scope(f"w{level}{chunk}{half}"):
                    level_copy(level, chunk, half).wait_recv()
            for n in range(2):
                merge(level, chunk, first_pair(level, half) + n)
        elif kind == "s":
            send(*numbers)
        else:
            need(4)
            need(5)
            with jax.named_scope(f"f{numbers[0]}"):
                finish(*numbers)

    for chunk in range(COUNT):
        with jax.named_scope(f"far{chunk}"):
            arrived = rb.at[pl.ds(0, PEERS - 1), pl.ds(PIECE_AT[chunk], PIECE_ROWS[chunk])]
            pltpu.make_async_copy(arrived, arrived, far_recv.at[chunk]).wait()
    with jax.named_scope("drain"):
        pltpu.make_async_copy(rb.at[0], rb.at[0], own_sem.at[0]).wait()
        sent = bx.at[pl.ds(0, PEERS - 1)]
        pltpu.make_async_copy(sent, sent, far_send.at[0]).wait()
        for level in range(LEVELS):
            for chunk in range(COUNT):
                moved = arrivals[level][chunk]
                pltpu.make_async_copy(moved, moved, lev_send.at[level, chunk]).wait()


def unpack(rb, out, ready, out_sem):
    groups = 4
    peers = PEERS // groups
    rows = peers * PIECE
    outs = [
        pltpu.make_async_copy(
            ready.at[pl.ds(g * rows, rows)], out.at[pl.ds(g * rows, rows)], out_sem.at[g]
        )
        for g in range(groups)
    ]
    step = min(PIECE_ROWS)
    lane = lax.broadcasted_iota(jnp.int32, (step, LANES), 1)
    for g in range(groups):
        for peer in range(g * peers, (g + 1) * peers):
            for block in range(0, COLS, LANES):
                for row in range(0, PIECE, step):
                    total = None
                    for chunk, (at, width) in enumerate(CHUNKS):
                        if not block <= at < block + LANES:
                            continue
                        group, inside = divmod(row, PIECE_ROWS[chunk])
                        first = PIECE_AT[chunk] + inside
                        part = rb[peer, first : first + step].astype(F32)
                        turn = (at - block - group * width) % LANES
                        part = pltpu.roll(part, turn, 1) if turn else part
                        mine = (lane >= at - block) & (lane < at - block + width)
                        total = part if total is None else jnp.where(mine, part, total)
                    base = peer * PIECE + row
                    ready[base : base + step, block : block + LANES] = total.astype(BF16)
        outs[g].start()
    with jax.named_scope("outs"):
        for copy in outs:
            copy.wait()


def on_device(vectors, leaf_basis, transfer, core_mats, row_basis, box_order):
    any_space = pl.BlockSpec(memory_space=pl.ANY)
    vmem = pl.BlockSpec(memory_space=pltpu.VMEM)
    call = pl.pallas_call(
        kernel,
        out_shape=pltpu.VMEM((PEERS, ALL_ROWS, LANES), BF16),
        in_specs=[any_space] * 5 + [pl.BlockSpec(memory_space=pltpu.SMEM)],
        out_specs=vmem,
        scratch_shapes=[
            pltpu.VMEM((BOXES * LEAF, COLS), BF16),
            pltpu.VMEM((BOXES * LEAF, RANK), BF16),
            pltpu.VMEM((LEVELS, BOXES, 2 * RANK, RANK), BF16),
            pltpu.VMEM((BOXES, RANK, RANK), BF16),
            pltpu.VMEM((BOXES * LEAF, RANK), BF16),
            pltpu.VMEM((PEERS, ALL_ROWS, LANES), BF16),
        ]
        + [pltpu.VMEM((BOXES, width, RANK), BF16) for _, width in CHUNKS] * (LEVELS + 1)
        + [pltpu.VMEM((HALF, width, RANK), BF16) for _, width in CHUNKS] * LEVELS
        + [pltpu.VMEM((BOXES, width, RANK), BF16) for _, width in CHUNKS]
        + [
            pltpu.SemaphoreType.DMA((10,)),
            pltpu.SemaphoreType.DMA((1,)),
            pltpu.SemaphoreType.DMA((LEVELS, COUNT)),
            pltpu.SemaphoreType.DMA((LEVELS, COUNT, 2)),
            pltpu.SemaphoreType.DMA((1,)),
            pltpu.SemaphoreType.DMA((COUNT,)),
        ],
        compiler_params=pltpu.CompilerParams(
            collective_id=0, has_side_effects=True, vmem_limit_bytes=KERNEL_VMEM
        ),
        name="butterfly",
    )
    arrived = call(
        vectors,
        leaf_basis,
        transfer.reshape(LEVELS, BOXES, 2 * RANK, RANK),
        core_mats.reshape(BOXES, RANK, RANK),
        row_basis,
        box_order.reshape(BOXES),
    )
    return pl.pallas_call(
        unpack,
        out_shape=jax.ShapeDtypeStruct((BOXES * LEAF, COLS), BF16),
        in_specs=[vmem],
        out_specs=any_space,
        scratch_shapes=[pltpu.VMEM((BOXES * LEAF, COLS), BF16), pltpu.SemaphoreType.DMA((4,))],
        compiler_params=pltpu.CompilerParams(vmem_limit_bytes=8 * 1024 * 1024),
        name="unpack",
    )(arrived)


def solution(mesh):
    in_specs = (
        P(("outer", "inner"), None),
        P(("outer", "inner"), None),
        P(None, "outer", "inner", None, None, None),
        P("outer", "inner", None, None, None),
        P(("outer", "inner"), None),
        P("outer", "inner", None),
    )
    out_specs = P(("outer", "inner"), None)
    return jax.shard_map(
        on_device, mesh=mesh, in_specs=in_specs, out_specs=out_specs, check_vma=False
    )
```

```python
import functools

import jax
import jax.numpy as jnp
from jax import lax
from jax.experimental import pallas as pl
from jax.experimental.pallas import tpu as pltpu
from jax.sharding import PartitionSpec as P

MESH = pl.DeviceIdType.MESH
F32 = jnp.float32
BF16 = jnp.bfloat16
LEVELS = 4
BOXES = 8
HALF = 4
RANK = 256
LEAF = 256
COLS = 256
CHUNKS = ((0, 32), (64, 64), (128, 64), (192, 64), (32, 32))
COUNT = len(CHUNKS)
LANES = 128
KERNEL_VMEM = 65_600_000
PEERS = 32
PIECE = BOXES * LEAF // PEERS
PIECE_ROWS = tuple(PIECE * width // LANES for _, width in CHUNKS)
PIECE_AT = tuple(sum(PIECE_ROWS[:c]) for c in range(COUNT))
ALL_ROWS = sum(PIECE_ROWS)

STEPS = (
    ("m", 0, 0, 0), ("s", 1, 0), ("m", 0, 0, 1), ("m", 0, 1, 0), ("s", 1, 1), ("m", 0, 1, 1),
    ("m", 0, 2, 0), ("s", 1, 2), ("m", 0, 2, 1), ("m", 0, 3, 0), ("s", 1, 3), ("m", 0, 3, 1),
    ("m", 0, 4, 0), ("s", 1, 4), ("m", 0, 4, 1), ("r", 1), ("m", 1, 0, 0), ("s", 2, 0),
    ("m", 1, 0, 1), ("r", 2), ("m", 1, 1, 0), ("h", 2, 1, 0), ("m", 2, 0, 0), ("s", 3, 0),
    ("h", 2, 1, 1), ("m", 1, 1, 1), ("m", 2, 0, 1), ("m", 1, 2, 0), ("m", 2, 1, 0),
    ("s", 3, 1), ("h", 2, 2, 0), ("h", 2, 2, 1), ("m", 1, 2, 1), ("m", 1, 3, 0), ("r", 3),
    ("m", 3, 0, 0), ("m", 3, 0, 1), ("f", 0), ("m", 1, 3, 1), ("m", 1, 4, 0), ("m", 1, 4, 1),
    ("m", 2, 1, 1), ("m", 2, 2, 0), ("s", 3, 2), ("h", 2, 3, 0), ("h", 2, 3, 1),
    ("h", 2, 4, 0), ("h", 2, 4, 1), ("m", 3, 1, 0), ("m", 3, 1, 1), ("f", 1), ("m", 2, 2, 1),
    ("m", 3, 2, 0), ("m", 3, 2, 1), ("f", 2), ("m", 2, 3, 0), ("s", 3, 3), ("m", 2, 3, 1),
    ("m", 2, 4, 0), ("s", 3, 4), ("m", 2, 4, 1), ("m", 3, 3, 0), ("m", 3, 3, 1), ("f", 3),
    ("m", 3, 4, 0), ("m", 3, 4, 1), ("f", 4),
)


def kernel(
    x_hbm, v_hbm, t_hbm, c_hbm, u_hbm, order_ref, rb,
    xv, vv, tv, cv, uv, bx, *rest,
):
    outer = lax.axis_index("outer")
    inner = lax.axis_index("inner")
    rest = list(rest)

    def take(count):
        taken, rest[:] = rest[:count], rest[count:]
        return taken

    states = [take(COUNT) for _ in range(LEVELS + 1)]
    arrivals = [take(COUNT) for _ in range(LEVELS)]
    cores = take(COUNT)
    in_sem, own_sem, lev_send, lev_recv, far_send, far_recv, ready = rest

    def bit(value, place):
        return lax.rem(lax.div(value, 1 << place), 2)

    flags = (bit(inner, 0), bit(inner, 1), bit(outer, 0), bit(outer, 1))
    partners = (
        (outer, inner + (1 - 2 * flags[0])),
        (outer, inner + 2 * (1 - 2 * flags[1])),
        (outer + (1 - 2 * flags[2]), inner),
        (outer + 2 * (1 - 2 * flags[3]), inner),
    )

    my_box = lax.div(inner, HALF)
    my_quarter = lax.rem(inner, HALF)
    my_x = lax.div(my_box, 4)
    my_pair = lax.rem(my_box, 4)
    boxes_order = []
    for pair_step in (2, 1, 3, 0):
        for x_step in (1, 0):
            box = lax.rem(my_x + x_step, 2) * 4 + lax.rem(my_pair + pair_step, 4)
            quarters = []
            for step in (1, 2, 3, 0):
                quarter = lax.rem(my_quarter + step, 4)
                is_self = pair_step == 0 and x_step == 0 and step == 0
                quarters.append((quarter, is_self))
            boxes_order.append((box, quarters))

    def half_rows(side):
        return pl.ds(pl.multiple_of(side * (HALF * LEAF), HALF * LEAF), HALF * LEAF)

    sent_rows, kept_rows = half_rows(1 - flags[0]), half_rows(flags[0])
    loads = [
        pltpu.make_async_copy(src, dst, in_sem.at[n])
        for n, (src, dst) in enumerate(
            (
                (t_hbm.at[0], tv.at[0]), (t_hbm.at[1], tv.at[1]),
                (t_hbm.at[2], tv.at[2]), (t_hbm.at[3], tv.at[3]),
                (c_hbm, cv), (u_hbm, uv),
                (x_hbm.at[sent_rows], xv.at[sent_rows]), (v_hbm.at[sent_rows], vv.at[sent_rows]),
                (x_hbm.at[kept_rows], xv.at[kept_rows]), (v_hbm.at[kept_rows], vv.at[kept_rows]),
            )
        )
    ]
    for n in (6, 7):
        loads[n].start()

    barrier = pltpu.get_barrier_semaphore()

    def place(x_step, z_step, core_step):
        x = lax.rem(lax.div(inner, 16) + x_step, 2)
        z = lax.rem(lax.div(inner, 2) + z_step + 8, 8)
        return outer, x * 16 + z * 2 + lax.rem(inner + core_step, 2)

    near = [place(0, 0, 1), place(0, 1, 0), place(0, -1, 0), place(1, 0, 0)]
    rounds = (
        near,
        [place(1, 0, 1), place(0, 2, 0), place(0, -2, 0)],
        [place(0, 0, 1), place(1, 0, 0), place(1, 0, 1)],
    )

    def signal(semaphore, devices):
        for device in devices:
            pl.semaphore_signal(semaphore, inc=1, device_id=device, device_id_type=MESH)

    signal(barrier, [*near, *partners[2:]])

    def first_pair(level, half):
        if level < LEVELS - 1:
            later = flags[level + 1]
            return 2 * (1 - later) if half == 0 else 2 * later
        return 2 * half

    def level_copy(level, chunk, half):
        halves = level in (1, 2)
        at, size = (first_pair(level, half), 2) if halves else (0, HALF)
        return pltpu.make_async_remote_copy(
            src_ref=states[level][chunk].at[pl.ds((1 - flags[level]) * HALF + at, size)],
            dst_ref=arrivals[level][chunk].at[pl.ds(at, size)],
            send_sem=lev_send.at[0],
            recv_sem=lev_recv.at[(0, 5, 15, 25)[level] + chunk + COUNT * half],
            device_id=partners[level],
            device_id_type=MESH,
        )

    def send(level, chunk):
        level_copy(level, chunk, 0).start()
        if level in (1, 2):
            level_copy(level, chunk, 1).start()

    def leaf(box):
        rows = pl.ds(pl.multiple_of(box * LEAF, LEAF), LEAF)
        made = lax.dot_general(
            xv[rows, :], vv[rows, :], (((0,), (0,)), ((), ())), preferred_element_type=F32
        ).astype(BF16)
        for chunk, (at, width) in enumerate(CHUNKS):
            states[0][chunk][box] = made[at : at + width]

    with jax.named_scope("load"):
        loads[6].wait()
        loads[7].wait()
    for n in (8, 9, 0):
        loads[n].start()
    for n in range(HALF):
        leaf((1 - flags[0]) * HALF + n)
    with jax.named_scope("greet"):
        pl.semaphore_wait(barrier, len(near) + 2)
    for chunk in range(COUNT):
        send(0, chunk)
    signal(ready.at[0], rounds[0])
    for n in (1, 2, 3, 4, 5):
        loads[n].start()
    loads[8].wait()
    loads[9].wait()
    for n in range(HALF):
        leaf(flags[0] * HALF + n)

    def merge(level, chunk, pair):
        flag = flags[level]
        kept = states[level][chunk][flag * HALF + pair]
        came = arrivals[level][chunk][pair]
        for o in range(2):
            box = 2 * pair + o
            kept_w = tv[level, box, pl.ds(pl.multiple_of(flag * RANK, RANK), RANK), :]
            came_w = tv[level, box, pl.ds(pl.multiple_of((1 - flag) * RANK, RANK), RANK), :]
            total = jnp.dot(kept, kept_w, preferred_element_type=F32)
            total = total + jnp.dot(came, came_w, preferred_element_type=F32)
            states[level + 1][chunk][box] = total.astype(BF16)

    def far_copy(chunk, box, quarter):
        peer = box * 4 + quarter
        rows = pl.ds(PIECE_AT[chunk], PIECE_ROWS[chunk])
        return pltpu.make_async_remote_copy(
            src_ref=bx.at[peer, rows],
            dst_ref=rb.at[inner, rows],
            send_sem=far_send.at[0],
            recv_sem=far_recv.at[chunk],
            device_id=(outer, peer),
            device_id_type=MESH,
        )

    own = [
        pltpu.make_async_copy(
            bx.at[inner, pl.ds(at, rows)], rb.at[inner, pl.ds(at, rows)], own_sem.at[0]
        )
        for at, rows in zip(PIECE_AT, PIECE_ROWS)
    ]

    def finish(chunk):
        size = PIECE_ROWS[chunk]
        at = PIECE_AT[chunk]
        core = cores[chunk]
        for part in (boxes_order,):
            for box, _ in part:
                core[box] = jnp.dot(
                    states[LEVELS][chunk][order_ref[box]], cv[box], preferred_element_type=F32
                ).astype(BF16)
            for box, _ in part:
                rows = pl.ds(pl.multiple_of(box * LEAF, LEAF), LEAF)
                made = jnp.dot(uv[rows, :], core[box].T, preferred_element_type=F32)
                for quarter in range(4):
                    groups = [
                        made[first : first + size]
                        for first in range(quarter * PIECE, (quarter + 1) * PIECE, size)
                    ]
                    bx[box * 4 + quarter, at : at + size] = jnp.concatenate(groups, axis=1).astype(BF16)
            for box, quarters in part:
                for quarter, is_self in quarters:
                    if is_self:
                        own[chunk].start()
                    else:
                        far_copy(chunk, box, quarter).start()

    loaded = set()

    def need(n):
        if n not in loaded:
            loaded.add(n)
            loads[n].wait()

    for kind, *numbers in STEPS:
        if kind == "m":
            level, chunk, half = numbers
            need(level)
            if half == 0 or level in (1, 2):
                with jax.named_scope(f"w{level}{chunk}{half}"):
                    level_copy(level, chunk, half).wait_recv()
            for n in range(2):
                merge(level, chunk, first_pair(level, half) + n)
        elif kind == "s":
            send(*numbers)
        elif kind == "h":
            level_copy(*numbers).start()
        elif kind == "r":
            (n,) = numbers
            with jax.named_scope(f"r{n}"):
                pl.semaphore_wait(ready.at[n - 1], len(rounds[n - 1]))
            if n < len(rounds):
                signal(ready.at[n], rounds[n])
        else:
            need(4)
            need(5)
            with jax.named_scope(f"f{numbers[0]}"):
                finish(*numbers)

    for chunk in range(COUNT):
        with jax.named_scope(f"far{chunk}"):
            arrived = rb.at[pl.ds(0, PEERS - 1), pl.ds(PIECE_AT[chunk], PIECE_ROWS[chunk])]
            pltpu.make_async_copy(arrived, arrived, far_recv.at[chunk]).wait()
    with jax.named_scope("drain"):
        pltpu.make_async_copy(rb.at[0], rb.at[0], own_sem.at[0]).wait()
        sent = bx.at[pl.ds(0, PEERS - 1)]
        pltpu.make_async_copy(sent, sent, far_send.at[0]).wait()
        pltpu.make_async_copy(tv.at[0], tv.at[0], lev_send.at[0]).wait()


def unpack(rb, out, ready, out_sem):
    groups = 4
    peers = PEERS // groups
    rows = peers * PIECE
    outs = [
        pltpu.make_async_copy(
            ready.at[pl.ds(g * rows, rows)], out.at[pl.ds(g * rows, rows)], out_sem.at[g]
        )
        for g in range(groups)
    ]
    step = min(PIECE_ROWS)
    lane = lax.broadcasted_iota(jnp.int32, (step, LANES), 1)
    for g in range(groups):
        for peer in range(g * peers, (g + 1) * peers):
            for block in range(0, COLS, LANES):
                for row in range(0, PIECE, step):
                    total = None
                    for chunk, (at, width) in enumerate(CHUNKS):
                        if not block <= at < block + LANES:
                            continue
                        group, inside = divmod(row, PIECE_ROWS[chunk])
                        first = PIECE_AT[chunk] + inside
                        part = rb[peer, first : first + step].astype(F32)
                        turn = (at - block - group * width) % LANES
                        part = pltpu.roll(part, turn, 1) if turn else part
                        mine = (lane >= at - block) & (lane < at - block + width)
                        total = part if total is None else jnp.where(mine, part, total)
                    base = peer * PIECE + row
                    ready[base : base + step, block : block + LANES] = total.astype(BF16)
        outs[g].start()
    with jax.named_scope("outs"):
        for copy in outs:
            copy.wait()


def on_device(vectors, leaf_basis, transfer, core_mats, row_basis, box_order):
    any_space = pl.BlockSpec(memory_space=pl.ANY)
    vmem = pl.BlockSpec(memory_space=pltpu.VMEM)
    call = pl.pallas_call(
        kernel,
        out_shape=pltpu.VMEM((PEERS, ALL_ROWS, LANES), BF16),
        in_specs=[any_space] * 5 + [pl.BlockSpec(memory_space=pltpu.SMEM)],
        out_specs=vmem,
        scratch_shapes=[
            pltpu.VMEM((BOXES * LEAF, COLS), BF16),
            pltpu.VMEM((BOXES * LEAF, RANK), BF16),
            pltpu.VMEM((LEVELS, BOXES, 2 * RANK, RANK), BF16),
            pltpu.VMEM((BOXES, RANK, RANK), BF16),
            pltpu.VMEM((BOXES * LEAF, RANK), BF16),
            pltpu.VMEM((PEERS, ALL_ROWS, LANES), BF16),
        ]
        + [pltpu.VMEM((BOXES, width, RANK), BF16) for _, width in CHUNKS] * (LEVELS + 1)
        + [pltpu.VMEM((HALF, width, RANK), BF16) for _, width in CHUNKS] * LEVELS
        + [pltpu.VMEM((BOXES, width, RANK), BF16) for _, width in CHUNKS]
        + [
            pltpu.SemaphoreType.DMA((10,)),
            pltpu.SemaphoreType.DMA((1,)),
            pltpu.SemaphoreType.DMA((1,)),
            pltpu.SemaphoreType.DMA((6 * COUNT,)),
            pltpu.SemaphoreType.DMA((1,)),
            pltpu.SemaphoreType.DMA((COUNT,)),
            pltpu.SemaphoreType.REGULAR((3,)),
        ],
        compiler_params=pltpu.CompilerParams(
            collective_id=0, has_side_effects=True, vmem_limit_bytes=KERNEL_VMEM
        ),
        name="butterfly",
    )
    arrived = call(
        vectors,
        leaf_basis,
        transfer.reshape(LEVELS, BOXES, 2 * RANK, RANK),
        core_mats.reshape(BOXES, RANK, RANK),
        row_basis,
        box_order.reshape(BOXES),
    )
    return pl.pallas_call(
        unpack,
        out_shape=jax.ShapeDtypeStruct((BOXES * LEAF, COLS), BF16),
        in_specs=[vmem],
        out_specs=any_space,
        scratch_shapes=[pltpu.VMEM((BOXES * LEAF, COLS), BF16), pltpu.SemaphoreType.DMA((4,))],
        compiler_params=pltpu.CompilerParams(vmem_limit_bytes=8 * 1024 * 1024),
        name="unpack",
    )(arrived)


def solution(mesh):
    in_specs = (
        P(("outer", "inner"), None),
        P(("outer", "inner"), None),
        P(None, "outer", "inner", None, None, None),
        P("outer", "inner", None, None, None),
        P(("outer", "inner"), None),
        P("outer", "inner", None),
    )
    out_specs = P(("outer", "inner"), None)
    return jax.shard_map(
        on_device, mesh=mesh, in_specs=in_specs, out_specs=out_specs, check_vma=False
    )
```

```python
import functools

import jax
import jax.numpy as jnp
from jax import lax
from jax.experimental import pallas as pl
from jax.experimental.pallas import tpu as pltpu
from jax.sharding import PartitionSpec as P

MESH = pl.DeviceIdType.MESH
F32 = jnp.float32
BF16 = jnp.bfloat16
LEVELS = 4
BOXES = 8
HALF = 4
RANK = 256
LEAF = 256
COLS = 256
CHUNKS = ((0, 32), (64, 64), (128, 64), (192, 64), (32, 32))
COUNT = len(CHUNKS)
LANES = 128
KERNEL_VMEM = 65_600_000
PEERS = 32
PIECE = BOXES * LEAF // PEERS
PIECE_ROWS = tuple(PIECE * width // LANES for _, width in CHUNKS)
PIECE_AT = tuple(sum(PIECE_ROWS[:c]) for c in range(COUNT))
ALL_ROWS = sum(PIECE_ROWS)

STEPS = (
    ("m", 0, 0, 0), ("s", 1, 0), ("m", 0, 0, 1), ("m", 0, 1, 0), ("s", 1, 1), ("m", 0, 1, 1),
    ("m", 0, 2, 0), ("s", 1, 2), ("m", 0, 2, 1), ("m", 0, 3, 0), ("s", 1, 3), ("m", 0, 3, 1),
    ("m", 0, 4, 0), ("s", 1, 4), ("m", 0, 4, 1), ("r", 1), ("m", 1, 0, 0), ("s", 2, 0),
    ("m", 1, 0, 1), ("r", 2), ("m", 1, 1, 0), ("h", 2, 1, 0), ("m", 2, 0, 0), ("s", 3, 0),
    ("h", 2, 1, 1), ("m", 1, 1, 1), ("m", 2, 0, 1), ("m", 1, 2, 0), ("m", 2, 1, 0),
    ("s", 3, 1), ("h", 2, 2, 0), ("h", 2, 2, 1), ("m", 1, 2, 1), ("m", 1, 3, 0), ("r", 3),
    ("m", 3, 0, 0), ("m", 3, 0, 1), ("f", 0), ("m", 1, 3, 1), ("m", 1, 4, 0), ("m", 2, 1, 1),
    ("m", 3, 1, 0), ("m", 3, 1, 1), ("m", 2, 2, 0), ("s", 3, 2), ("f", 1), ("h", 2, 3, 0),
    ("h", 2, 3, 1), ("m", 1, 4, 1), ("m", 2, 2, 1), ("m", 2, 3, 0), ("s", 3, 3),
    ("h", 2, 4, 0), ("h", 2, 4, 1), ("m", 3, 2, 0), ("m", 3, 2, 1), ("f", 2), ("m", 2, 3, 1),
    ("m", 2, 4, 0), ("s", 3, 4), ("m", 2, 4, 1), ("m", 3, 3, 0), ("m", 3, 3, 1), ("f", 3),
    ("m", 3, 4, 0), ("m", 3, 4, 1), ("f", 4),
)


def kernel(
    x_hbm, v_hbm, t_hbm, c_hbm, u_hbm, order_hbm, rb,
    xv, vv, tv, cv, uv, bx, order_ref, *rest,
):
    outer = lax.axis_index("outer")
    inner = lax.axis_index("inner")
    rest = list(rest)

    def take(count):
        taken, rest[:] = rest[:count], rest[count:]
        return taken

    states = [take(COUNT) for _ in range(LEVELS + 1)]
    arrivals = [take(COUNT) for _ in range(LEVELS)]
    cores = take(COUNT)
    in_sem, own_sem, lev_send, lev_recv, far_send, far_recv, ready = rest

    def bit(value, place):
        return lax.rem(lax.div(value, 1 << place), 2)

    flags = (bit(inner, 0), bit(inner, 1), bit(outer, 0), bit(outer, 1))
    partners = (
        (outer, inner + (1 - 2 * flags[0])),
        (outer, inner + 2 * (1 - 2 * flags[1])),
        (outer + (1 - 2 * flags[2]), inner),
        (outer + 2 * (1 - 2 * flags[3]), inner),
    )

    my_box = lax.div(inner, HALF)
    my_quarter = lax.rem(inner, HALF)
    my_x = lax.div(my_box, 4)
    my_pair = lax.rem(my_box, 4)
    boxes_order = []
    for pair_step in (2, 1, 3, 0):
        for x_step in (1, 0):
            box = lax.rem(my_x + x_step, 2) * 4 + lax.rem(my_pair + pair_step, 4)
            quarters = []
            for step in (1, 2, 3, 0):
                quarter = lax.rem(my_quarter + step, 4)
                is_self = pair_step == 0 and x_step == 0 and step == 0
                quarters.append((quarter, is_self))
            boxes_order.append((box, quarters))

    def half_rows(side):
        return pl.ds(pl.multiple_of(side * (HALF * LEAF), HALF * LEAF), HALF * LEAF)

    sent_rows, kept_rows = half_rows(1 - flags[0]), half_rows(flags[0])
    loads = [
        pltpu.make_async_copy(src, dst, in_sem.at[n])
        for n, (src, dst) in enumerate(
            (
                (t_hbm.at[0], tv.at[0]), (t_hbm.at[1], tv.at[1]),
                (t_hbm.at[2], tv.at[2]), (t_hbm.at[3], tv.at[3]),
                (c_hbm, cv), (u_hbm, uv),
                (x_hbm.at[sent_rows], xv.at[sent_rows]), (v_hbm.at[sent_rows], vv.at[sent_rows]),
                (x_hbm.at[kept_rows], xv.at[kept_rows]), (v_hbm.at[kept_rows], vv.at[kept_rows]),
                (order_hbm, order_ref),
            )
        )
    ]
    for n in (6, 7, 8, 9):
        loads[n].start()

    barrier = pltpu.get_barrier_semaphore()

    def place(x_step, z_step, core_step):
        x = lax.rem(lax.div(inner, 16) + x_step, 2)
        z = lax.rem(lax.div(inner, 2) + z_step + 8, 8)
        return outer, x * 16 + z * 2 + lax.rem(inner + core_step, 2)

    near = [place(0, 0, 1), place(0, 1, 0), place(0, -1, 0), place(1, 0, 0)]
    y_high, y = outer - lax.rem(outer, 4), lax.rem(outer, 4)
    y_near = [(y_high + lax.rem(y + step, 4), inner) for step in (1, 3)]
    rounds = (
        [*near, partners[2]],
        [place(1, 0, 1), place(0, 2, 0), place(0, -2, 0)],
        [place(0, 0, 1), place(1, 0, 0), place(1, 0, 1)],
    )

    def signal(semaphore, devices):
        for device in devices:
            pl.semaphore_signal(semaphore, inc=1, device_id=device, device_id_type=MESH)

    signal(barrier, [*near, *y_near])
    for n in (0, 10):
        loads[n].start()

    def first_pair(level, half):
        if level < LEVELS - 1:
            later = flags[level + 1]
            return 2 * (1 - later) if half == 0 else 2 * later
        return 2 * half

    def level_copy(level, chunk, half):
        halves = level in (1, 2)
        at, size = (first_pair(level, half), 2) if halves else (0, HALF)
        return pltpu.make_async_remote_copy(
            src_ref=states[level][chunk].at[pl.ds((1 - flags[level]) * HALF + at, size)],
            dst_ref=arrivals[level][chunk].at[pl.ds(at, size)],
            send_sem=lev_send.at[0],
            recv_sem=lev_recv.at[(0, 5, 15, 25)[level] + chunk + COUNT * half],
            device_id=partners[level],
            device_id_type=MESH,
        )

    def send(level, chunk):
        level_copy(level, chunk, 0).start()
        if level in (1, 2):
            level_copy(level, chunk, 1).start()

    def leaf(box):
        rows = pl.ds(pl.multiple_of(box * LEAF, LEAF), LEAF)
        made = lax.dot_general(
            xv[rows, :], vv[rows, :], (((0,), (0,)), ((), ())), preferred_element_type=F32
        ).astype(BF16)
        for chunk, (at, width) in enumerate(CHUNKS):
            states[0][chunk][box] = made[at : at + width]

    with jax.named_scope("load"):
        loads[6].wait()
        loads[7].wait()
    for n in range(HALF):
        leaf((1 - flags[0]) * HALF + n)
    with jax.named_scope("greet"):
        pl.semaphore_wait(barrier, len(near) + 2)
    for chunk in range(COUNT):
        send(0, chunk)
    signal(ready.at[0], rounds[0])
    for n in (1, 2, 3, 4, 5):
        loads[n].start()
    loads[8].wait()
    loads[9].wait()
    for n in range(HALF):
        leaf(flags[0] * HALF + n)

    def merge(level, chunk, pair):
        flag = flags[level]
        kept = states[level][chunk][flag * HALF + pair]
        came = arrivals[level][chunk][pair]
        for o in range(2):
            box = 2 * pair + o
            kept_w = tv[level, box, pl.ds(pl.multiple_of(flag * RANK, RANK), RANK), :]
            came_w = tv[level, box, pl.ds(pl.multiple_of((1 - flag) * RANK, RANK), RANK), :]
            total = jnp.dot(kept, kept_w, preferred_element_type=F32)
            total = total + jnp.dot(came, came_w, preferred_element_type=F32)
            states[level + 1][chunk][box] = total.astype(BF16)

    def far_copy(chunk, box, quarter):
        peer = box * 4 + quarter
        rows = pl.ds(PIECE_AT[chunk], PIECE_ROWS[chunk])
        return pltpu.make_async_remote_copy(
            src_ref=bx.at[peer, rows],
            dst_ref=rb.at[inner, rows],
            send_sem=far_send.at[0],
            recv_sem=far_recv.at[chunk],
            device_id=(outer, peer),
            device_id_type=MESH,
        )

    own = [
        pltpu.make_async_copy(
            bx.at[inner, pl.ds(at, rows)], rb.at[inner, pl.ds(at, rows)], own_sem.at[0]
        )
        for at, rows in zip(PIECE_AT, PIECE_ROWS)
    ]

    def finish(chunk):
        size = PIECE_ROWS[chunk]
        at = PIECE_AT[chunk]
        core = cores[chunk]
        for part in (boxes_order,):
            for box, _ in part:
                core[box] = jnp.dot(
                    states[LEVELS][chunk][order_ref[box]], cv[box], preferred_element_type=F32
                ).astype(BF16)
            for box, _ in part:
                rows = pl.ds(pl.multiple_of(box * LEAF, LEAF), LEAF)
                made = jnp.dot(uv[rows, :], core[box].T, preferred_element_type=F32)
                for quarter in range(4):
                    groups = [
                        made[first : first + size]
                        for first in range(quarter * PIECE, (quarter + 1) * PIECE, size)
                    ]
                    bx[box * 4 + quarter, at : at + size] = jnp.concatenate(groups, axis=1).astype(BF16)
            for box, quarters in part:
                for quarter, is_self in quarters:
                    if is_self:
                        own[chunk].start()
                    else:
                        far_copy(chunk, box, quarter).start()

    loaded = set()

    def need(n):
        if n not in loaded:
            loaded.add(n)
            loads[n].wait()

    for kind, *numbers in STEPS:
        if kind == "m":
            level, chunk, half = numbers
            need(level)
            if half == 0 or level in (1, 2):
                with jax.named_scope(f"w{level}{chunk}{half}"):
                    level_copy(level, chunk, half).wait_recv()
            for n in range(2):
                merge(level, chunk, first_pair(level, half) + n)
        elif kind == "s":
            send(*numbers)
        elif kind == "h":
            level_copy(*numbers).start()
        elif kind == "r":
            (n,) = numbers
            with jax.named_scope(f"r{n}"):
                pl.semaphore_wait(ready.at[n - 1], len(rounds[n - 1]))
            if n < len(rounds):
                signal(ready.at[n], rounds[n])
        else:
            need(4)
            need(5)
            need(10)
            with jax.named_scope(f"f{numbers[0]}"):
                finish(*numbers)

    for chunk in range(COUNT):
        with jax.named_scope(f"far{chunk}"):
            arrived = rb.at[pl.ds(0, PEERS - 1), pl.ds(PIECE_AT[chunk], PIECE_ROWS[chunk])]
            pltpu.make_async_copy(arrived, arrived, far_recv.at[chunk]).wait()
    with jax.named_scope("drain"):
        pltpu.make_async_copy(rb.at[0], rb.at[0], own_sem.at[0]).wait()
        sent = bx.at[pl.ds(0, PEERS - 1)]
        pltpu.make_async_copy(sent, sent, far_send.at[0]).wait()
        pltpu.make_async_copy(tv.at[0], tv.at[0], lev_send.at[0]).wait()


def unpack(rb, out, ready, out_sem):
    groups = 4
    peers = PEERS // groups
    rows = peers * PIECE
    outs = [
        pltpu.make_async_copy(
            ready.at[pl.ds(g * rows, rows)], out.at[pl.ds(g * rows, rows)], out_sem.at[g]
        )
        for g in range(groups)
    ]
    step = min(PIECE_ROWS)
    lane = lax.broadcasted_iota(jnp.int32, (step, LANES), 1)
    for g in range(groups):
        for peer in range(g * peers, (g + 1) * peers):
            for block in range(0, COLS, LANES):
                for row in range(0, PIECE, step):
                    total = None
                    for chunk, (at, width) in enumerate(CHUNKS):
                        if not block <= at < block + LANES:
                            continue
                        group, inside = divmod(row, PIECE_ROWS[chunk])
                        first = PIECE_AT[chunk] + inside
                        part = rb[peer, first : first + step].astype(F32)
                        turn = (at - block - group * width) % LANES
                        part = pltpu.roll(part, turn, 1) if turn else part
                        mine = (lane >= at - block) & (lane < at - block + width)
                        total = part if total is None else jnp.where(mine, part, total)
                    base = peer * PIECE + row
                    ready[base : base + step, block : block + LANES] = total.astype(BF16)
        outs[g].start()
    with jax.named_scope("outs"):
        for copy in outs:
            copy.wait()


def on_device(vectors, leaf_basis, transfer, core_mats, row_basis, box_order):
    any_space = pl.BlockSpec(memory_space=pl.ANY)
    vmem = pl.BlockSpec(memory_space=pltpu.VMEM)
    call = pl.pallas_call(
        kernel,
        out_shape=pltpu.VMEM((PEERS, ALL_ROWS, LANES), BF16),
        in_specs=[any_space] * 6,
        out_specs=vmem,
        scratch_shapes=[
            pltpu.VMEM((BOXES * LEAF, COLS), BF16),
            pltpu.VMEM((BOXES * LEAF, RANK), BF16),
            pltpu.VMEM((LEVELS, BOXES, 2 * RANK, RANK), BF16),
            pltpu.VMEM((BOXES, RANK, RANK), BF16),
            pltpu.VMEM((BOXES * LEAF, RANK), BF16),
            pltpu.VMEM((PEERS, ALL_ROWS, LANES), BF16),
            pltpu.SMEM((BOXES,), jnp.int32),
        ]
        + [pltpu.VMEM((BOXES, width, RANK), BF16) for _, width in CHUNKS] * (LEVELS + 1)
        + [pltpu.VMEM((HALF, width, RANK), BF16) for _, width in CHUNKS] * LEVELS
        + [pltpu.VMEM((BOXES, width, RANK), BF16) for _, width in CHUNKS]
        + [
            pltpu.SemaphoreType.DMA((11,)),
            pltpu.SemaphoreType.DMA((1,)),
            pltpu.SemaphoreType.DMA((1,)),
            pltpu.SemaphoreType.DMA((6 * COUNT,)),
            pltpu.SemaphoreType.DMA((1,)),
            pltpu.SemaphoreType.DMA((COUNT,)),
            pltpu.SemaphoreType.REGULAR((3,)),
        ],
        compiler_params=pltpu.CompilerParams(
            collective_id=0, has_side_effects=True, vmem_limit_bytes=KERNEL_VMEM
        ),
        name="butterfly",
    )
    arrived = call(
        vectors,
        leaf_basis,
        transfer.reshape(LEVELS, BOXES, 2 * RANK, RANK),
        core_mats.reshape(BOXES, RANK, RANK),
        row_basis,
        box_order.reshape(BOXES),
    )
    return pl.pallas_call(
        unpack,
        out_shape=jax.ShapeDtypeStruct((BOXES * LEAF, COLS), BF16),
        in_specs=[vmem],
        out_specs=any_space,
        scratch_shapes=[pltpu.VMEM((BOXES * LEAF, COLS), BF16), pltpu.SemaphoreType.DMA((4,))],
        compiler_params=pltpu.CompilerParams(vmem_limit_bytes=8 * 1024 * 1024),
        name="unpack",
    )(arrived)


def solution(mesh):
    in_specs = (
        P(("outer", "inner"), None),
        P(("outer", "inner"), None),
        P(None, "outer", "inner", None, None, None),
        P("outer", "inner", None, None, None),
        P(("outer", "inner"), None),
        P("outer", "inner", None),
    )
    out_specs = P(("outer", "inner"), None)
    return jax.shard_map(
        on_device, mesh=mesh, in_specs=in_specs, out_specs=out_specs, check_vma=False
    )
```

```python
import functools

import jax
import jax.numpy as jnp
from jax import lax
from jax.experimental import pallas as pl
from jax.experimental.pallas import tpu as pltpu
from jax.sharding import PartitionSpec as P

MESH = pl.DeviceIdType.MESH
F32 = jnp.float32
BF16 = jnp.bfloat16
LEVELS = 4
BOXES = 8
HALF = 4
RANK = 256
LEAF = 256
COLS = 256
CHUNKS = ((0, 32), (64, 64), (128, 64), (192, 64), (32, 32))
COUNT = len(CHUNKS)
LANES = 128
KERNEL_VMEM = 65_100_000
PEERS = 32
PIECE = BOXES * LEAF // PEERS
PIECE_ROWS = tuple(PIECE * width // LANES for _, width in CHUNKS)
PIECE_AT = tuple(sum(PIECE_ROWS[:c]) for c in range(COUNT))
ALL_ROWS = sum(PIECE_ROWS)

STEPS = (
    ("m", 0, 0, 0), ("s", 1, 0), ("m", 0, 0, 1), ("m", 0, 1, 0), ("s", 1, 1), ("m", 0, 1, 1),
    ("m", 0, 2, 0), ("s", 1, 2), ("m", 0, 2, 1), ("m", 0, 3, 0), ("s", 1, 3), ("m", 0, 3, 1),
    ("m", 0, 4, 0), ("s", 1, 4), ("m", 0, 4, 1), ("r", 1), ("m", 1, 0, 0), ("s", 2, 0),
    ("m", 1, 0, 1), ("r", 2), ("m", 1, 1, 0), ("h", 2, 1, 0), ("m", 2, 0, 0), ("s", 3, 0),
    ("h", 2, 1, 1), ("m", 1, 1, 1), ("m", 2, 0, 1), ("m", 1, 2, 0), ("m", 2, 1, 0),
    ("s", 3, 1), ("h", 2, 2, 0), ("h", 2, 2, 1), ("m", 1, 2, 1), ("m", 1, 3, 0), ("r", 3),
    ("m", 3, 0, 0), ("m", 3, 0, 1), ("f", 0), ("m", 1, 3, 1), ("m", 1, 4, 0), ("m", 2, 1, 1),
    ("m", 3, 1, 0), ("m", 3, 1, 1), ("m", 2, 2, 0), ("s", 3, 2), ("f", 1), ("h", 2, 3, 0),
    ("h", 2, 3, 1), ("m", 1, 4, 1), ("m", 2, 2, 1), ("m", 2, 3, 0), ("s", 3, 3),
    ("h", 2, 4, 0), ("h", 2, 4, 1), ("m", 3, 2, 0), ("m", 3, 2, 1), ("f", 2), ("m", 2, 3, 1),
    ("m", 2, 4, 0), ("s", 3, 4), ("m", 2, 4, 1), ("m", 3, 3, 0), ("m", 3, 3, 1), ("f", 3),
    ("m", 3, 4, 0), ("m", 3, 4, 1), ("f", 4),
)


def kernel(
    x_hbm, v_hbm, t_hbm, c_hbm, u_hbm, order_hbm, rb, flat,
    xv, vv, tv, cv, uv, bx, order_ref, *rest,
):
    outer = lax.axis_index("outer")
    inner = lax.axis_index("inner")
    rest = list(rest)

    def take(count):
        taken, rest[:] = rest[:count], rest[count:]
        return taken

    states = [take(COUNT) for _ in range(LEVELS + 1)]
    arrivals = [take(COUNT) for _ in range(LEVELS)]
    cores = take(COUNT)
    in_sem, own_sem, lev_send, lev_recv, far_send, far_recv, ready = rest

    def bit(value, place):
        return lax.rem(lax.div(value, 1 << place), 2)

    flags = (bit(inner, 0), bit(inner, 1), bit(outer, 0), bit(outer, 1))
    partners = (
        (outer, inner + (1 - 2 * flags[0])),
        (outer, inner + 2 * (1 - 2 * flags[1])),
        (outer + (1 - 2 * flags[2]), inner),
        (outer + 2 * (1 - 2 * flags[3]), inner),
    )

    my_box = lax.div(inner, HALF)
    my_quarter = lax.rem(inner, HALF)
    my_x = lax.div(my_box, 4)
    my_pair = lax.rem(my_box, 4)
    boxes_order = []
    for pair_step in (2, 1, 3, 0):
        for x_step in (1, 0):
            box = lax.rem(my_x + x_step, 2) * 4 + lax.rem(my_pair + pair_step, 4)
            quarters = []
            for step in (1, 2, 3, 0):
                quarter = lax.rem(my_quarter + step, 4)
                is_self = pair_step == 0 and x_step == 0 and step == 0
                quarters.append((quarter, is_self))
            boxes_order.append((box, quarters))

    def half_rows(side):
        return pl.ds(pl.multiple_of(side * (HALF * LEAF), HALF * LEAF), HALF * LEAF)

    sent_rows, kept_rows = half_rows(1 - flags[0]), half_rows(flags[0])
    loads = [
        pltpu.make_async_copy(src, dst, in_sem.at[n])
        for n, (src, dst) in enumerate(
            (
                (t_hbm.at[0], tv.at[0]), (t_hbm.at[1], tv.at[1]),
                (t_hbm.at[2], tv.at[2]), (t_hbm.at[3], tv.at[3]),
                (c_hbm, cv), (u_hbm, uv),
                (x_hbm.at[sent_rows], xv.at[sent_rows]), (v_hbm.at[sent_rows], vv.at[sent_rows]),
                (x_hbm.at[kept_rows], xv.at[kept_rows]), (v_hbm.at[kept_rows], vv.at[kept_rows]),
                (order_hbm, order_ref),
            )
        )
    ]
    for n in (6, 7, 8, 9):
        loads[n].start()

    barrier = pltpu.get_barrier_semaphore()

    def place(x_step, z_step, core_step):
        x = lax.rem(lax.div(inner, 16) + x_step, 2)
        z = lax.rem(lax.div(inner, 2) + z_step + 8, 8)
        return outer, x * 16 + z * 2 + lax.rem(inner + core_step, 2)

    near = [place(0, 0, 1), place(0, 1, 0), place(0, -1, 0), place(1, 0, 0)]
    y_high, y = outer - lax.rem(outer, 4), lax.rem(outer, 4)
    y_near = [(y_high + lax.rem(y + step, 4), inner) for step in (1, 3)]
    rounds = (
        [*near, partners[2]],
        [place(1, 0, 1), place(0, 2, 0), place(0, -2, 0)],
        [place(0, 0, 1), place(1, 0, 0), place(1, 0, 1)],
    )

    def signal(semaphore, devices):
        for device in devices:
            pl.semaphore_signal(semaphore, inc=1, device_id=device, device_id_type=MESH)

    signal(barrier, [*near, *y_near])
    for n in (0, 10):
        loads[n].start()

    def first_pair(level, half):
        if level < LEVELS - 1:
            later = flags[level + 1]
            return 2 * (1 - later) if half == 0 else 2 * later
        return 2 * half

    def level_copy(level, chunk, half):
        halves = level in (1, 2)
        at, size = (first_pair(level, half), 2) if halves else (0, HALF)
        return pltpu.make_async_remote_copy(
            src_ref=states[level][chunk].at[pl.ds((1 - flags[level]) * HALF + at, size)],
            dst_ref=arrivals[level][chunk].at[pl.ds(at, size)],
            send_sem=lev_send.at[0],
            recv_sem=lev_recv.at[(0, 5, 15, 25)[level] + chunk + COUNT * half],
            device_id=partners[level],
            device_id_type=MESH,
        )

    def send(level, chunk):
        level_copy(level, chunk, 0).start()
        if level in (1, 2):
            level_copy(level, chunk, 1).start()

    def leaf(box):
        rows = pl.ds(pl.multiple_of(box * LEAF, LEAF), LEAF)
        made = lax.dot_general(
            xv[rows, :], vv[rows, :], (((0,), (0,)), ((), ())), preferred_element_type=F32
        ).astype(BF16)
        for chunk, (at, width) in enumerate(CHUNKS):
            states[0][chunk][box] = made[at : at + width]

    with jax.named_scope("load"):
        loads[6].wait()
        loads[7].wait()
    for n in range(HALF):
        leaf((1 - flags[0]) * HALF + n)
    with jax.named_scope("greet"):
        pl.semaphore_wait(barrier, len(near) + 2)
    for chunk in range(COUNT):
        send(0, chunk)
    signal(ready.at[0], rounds[0])
    for n in (1, 2, 3, 4, 5):
        loads[n].start()
    loads[8].wait()
    loads[9].wait()
    for n in range(HALF):
        leaf(flags[0] * HALF + n)

    def merge(level, chunk, pair):
        flag = flags[level]
        kept = states[level][chunk][flag * HALF + pair]
        came = arrivals[level][chunk][pair]
        for o in range(2):
            box = 2 * pair + o
            kept_w = tv[level, box, pl.ds(pl.multiple_of(flag * RANK, RANK), RANK), :]
            came_w = tv[level, box, pl.ds(pl.multiple_of((1 - flag) * RANK, RANK), RANK), :]
            total = jnp.dot(kept, kept_w, preferred_element_type=F32)
            total = total + jnp.dot(came, came_w, preferred_element_type=F32)
            states[level + 1][chunk][box] = total.astype(BF16)

    def far_copy(chunk, box, quarter):
        peer = box * 4 + quarter
        rows = pl.ds(PIECE_AT[chunk], PIECE_ROWS[chunk])
        return pltpu.make_async_remote_copy(
            src_ref=bx.at[peer, rows],
            dst_ref=rb.at[inner, rows],
            send_sem=far_send.at[0],
            recv_sem=far_recv.at[chunk],
            device_id=(outer, peer),
            device_id_type=MESH,
        )

    own = [
        pltpu.make_async_copy(
            bx.at[inner, pl.ds(at, rows)], rb.at[inner, pl.ds(at, rows)], own_sem.at[0]
        )
        for at, rows in zip(PIECE_AT, PIECE_ROWS)
    ]

    def finish(chunk):
        size = PIECE_ROWS[chunk]
        at = PIECE_AT[chunk]
        core = cores[chunk]
        for part in (boxes_order,):
            for box, _ in part:
                core[box] = jnp.dot(
                    states[LEVELS][chunk][order_ref[box]], cv[box], preferred_element_type=F32
                ).astype(BF16)
            for box, _ in part:
                rows = pl.ds(pl.multiple_of(box * LEAF, LEAF), LEAF)
                made = jnp.dot(uv[rows, :], core[box].T, preferred_element_type=F32)
                for quarter in range(4):
                    groups = [
                        made[first : first + size]
                        for first in range(quarter * PIECE, (quarter + 1) * PIECE, size)
                    ]
                    bx[box * 4 + quarter, at : at + size] = jnp.concatenate(groups, axis=1).astype(BF16)
            for box, quarters in part:
                for quarter, is_self in quarters:
                    if is_self:
                        own[chunk].start()
                    else:
                        far_copy(chunk, box, quarter).start()

    loaded = set()

    def need(n):
        if n not in loaded:
            loaded.add(n)
            loads[n].wait()

    for kind, *numbers in STEPS:
        if kind == "m":
            level, chunk, half = numbers
            need(level)
            if half == 0 or level in (1, 2):
                with jax.named_scope(f"w{level}{chunk}{half}"):
                    level_copy(level, chunk, half).wait_recv()
            for n in range(2):
                merge(level, chunk, first_pair(level, half) + n)
        elif kind == "s":
            send(*numbers)
        elif kind == "h":
            level_copy(*numbers).start()
        elif kind == "r":
            (n,) = numbers
            with jax.named_scope(f"r{n}"):
                pl.semaphore_wait(ready.at[n - 1], len(rounds[n - 1]))
            if n < len(rounds):
                signal(ready.at[n], rounds[n])
        else:
            need(4)
            need(5)
            need(10)
            with jax.named_scope(f"f{numbers[0]}"):
                finish(*numbers)

    for chunk in range(COUNT):
        with jax.named_scope(f"far{chunk}"):
            arrived = rb.at[pl.ds(0, PEERS - 1), pl.ds(PIECE_AT[chunk], PIECE_ROWS[chunk])]
            pltpu.make_async_copy(arrived, arrived, far_recv.at[chunk]).wait()
        if chunk == COUNT - 2:
            pltpu.make_async_copy(rb.at[0], rb.at[0], own_sem.at[0]).wait()
            for peer in range(PEERS):
                lay_out(rb, flat, peer, LANES)
    with jax.named_scope("drain"):
        sent = bx.at[pl.ds(0, PEERS - 1)]
        pltpu.make_async_copy(sent, sent, far_send.at[0]).wait()
        pltpu.make_async_copy(tv.at[0], tv.at[0], lev_send.at[0]).wait()


def lay_out(rb, target, peer, block):
    step = min(PIECE_ROWS)
    lane = lax.broadcasted_iota(jnp.int32, (step, LANES), 1)
    for row in range(0, PIECE, step):
        total = None
        for chunk, (at, width) in enumerate(CHUNKS):
            if not block <= at < block + LANES:
                continue
            group, inside = divmod(row, PIECE_ROWS[chunk])
            first = PIECE_AT[chunk] + inside
            part = rb[peer, first : first + step].astype(F32)
            turn = (at - block - group * width) % LANES
            part = pltpu.roll(part, turn, 1) if turn else part
            mine = (lane >= at - block) & (lane < at - block + width)
            total = part if total is None else jnp.where(mine, part, total)
        base = peer * PIECE + row
        target[base : base + step, :] = total.astype(BF16)


def unpack(rb, flat, out, ready, out_sem):
    groups = 4
    peers = PEERS // groups
    rows = peers * PIECE
    outs = [
        pltpu.make_async_copy(
            ready.at[pl.ds(g * rows, rows)],
            out.at[pl.ds(g * rows, rows), pl.ds(0, LANES)],
            out_sem.at[g],
        )
        for g in range(groups)
    ]
    outs.append(pltpu.make_async_copy(flat, out.at[:, pl.ds(LANES, LANES)], out_sem.at[groups]))
    outs[groups].start()
    for g in range(groups):
        for peer in range(g * peers, (g + 1) * peers):
            lay_out(rb, ready, peer, 0)
        outs[g].start()
    for copy in outs:
        copy.wait()


def on_device(vectors, leaf_basis, transfer, core_mats, row_basis, box_order):
    any_space = pl.BlockSpec(memory_space=pl.ANY)
    vmem = pl.BlockSpec(memory_space=pltpu.VMEM)
    call = pl.pallas_call(
        kernel,
        out_shape=(
            pltpu.VMEM((PEERS, ALL_ROWS, LANES), BF16),
            pltpu.VMEM((BOXES * LEAF, LANES), BF16),
        ),
        in_specs=[any_space] * 6,
        out_specs=(vmem, vmem),
        scratch_shapes=[
            pltpu.VMEM((BOXES * LEAF, COLS), BF16),
            pltpu.VMEM((BOXES * LEAF, RANK), BF16),
            pltpu.VMEM((LEVELS, BOXES, 2 * RANK, RANK), BF16),
            pltpu.VMEM((BOXES, RANK, RANK), BF16),
            pltpu.VMEM((BOXES * LEAF, RANK), BF16),
            pltpu.VMEM((PEERS, ALL_ROWS, LANES), BF16),
            pltpu.SMEM((BOXES,), jnp.int32),
        ]
        + [pltpu.VMEM((BOXES, width, RANK), BF16) for _, width in CHUNKS] * (LEVELS + 1)
        + [pltpu.VMEM((HALF, width, RANK), BF16) for _, width in CHUNKS] * LEVELS
        + [pltpu.VMEM((BOXES, width, RANK), BF16) for _, width in CHUNKS]
        + [
            pltpu.SemaphoreType.DMA((11,)),
            pltpu.SemaphoreType.DMA((1,)),
            pltpu.SemaphoreType.DMA((1,)),
            pltpu.SemaphoreType.DMA((6 * COUNT,)),
            pltpu.SemaphoreType.DMA((1,)),
            pltpu.SemaphoreType.DMA((COUNT,)),
            pltpu.SemaphoreType.REGULAR((3,)),
        ],
        compiler_params=pltpu.CompilerParams(
            collective_id=0, has_side_effects=True, vmem_limit_bytes=KERNEL_VMEM
        ),
        name="butterfly",
    )
    arrived, flat = call(
        vectors,
        leaf_basis,
        transfer.reshape(LEVELS, BOXES, 2 * RANK, RANK),
        core_mats.reshape(BOXES, RANK, RANK),
        row_basis,
        box_order.reshape(BOXES),
    )
    return pl.pallas_call(
        unpack,
        out_shape=jax.ShapeDtypeStruct((BOXES * LEAF, COLS), BF16),
        in_specs=[vmem, vmem],
        out_specs=any_space,
        scratch_shapes=[pltpu.VMEM((BOXES * LEAF, LANES), BF16), pltpu.SemaphoreType.DMA((5,))],
        compiler_params=pltpu.CompilerParams(vmem_limit_bytes=8 * 1024 * 1024),
        name="unpack",
    )(arrived, flat)


def solution(mesh):
    in_specs = (
        P(("outer", "inner"), None),
        P(("outer", "inner"), None),
        P(None, "outer", "inner", None, None, None),
        P("outer", "inner", None, None, None),
        P(("outer", "inner"), None),
        P("outer", "inner", None),
    )
    out_specs = P(("outer", "inner"), None)
    return jax.shard_map(
        on_device, mesh=mesh, in_specs=in_specs, out_specs=out_specs, check_vma=False
    )
```
